256 devices in a mesh: dp: 64 (over z, y, x_hi), mp: 4 (over x_lo, core).
Axes of the slice: x: 4 (x_hi: 2, x_lo: 2; x = x_hi * 2 + x_lo), y: 4, z: 8, core: 2. Of those that a mesh axis runs over, the one named last changes fastest.
Arguments:
- streams: bfloat16 [16384, 4, 8192], P('dp', None, 'mp'), may hold values from -200 to 200
- branch_out: bfloat16 [16384, 8192], P('dp', 'mp'), may hold values from -6 to 6
- merge_weight: float32 [20, 4, 8192], P(None, None, ('mp', 'dp')), may hold values from -0.03125 to 0.03125
- next_weight: float32 [24, 4, 8192], P(None, None, ('mp', 'dp')), may hold values from -0.03125 to 0.03125
- blend_bias: float32 [44], replicated, may hold values from -3 to 3
- blend_scale: float32 [5], replicated, may hold values from 0.5 to 3
- norm_gain: float32 [8192], P('mp'), may hold values from 0.5 to 1.5
Outputs:
- streams_out: bfloat16 [16384, 4, 8192], P('dp', None, 'mp')
- branch_in: bfloat16 [16384, 8192], P('dp', 'mp')
- next_mix: float32 [16384, 20], P('dp')
The draws below stay inside these ranges and needn't reach their ends.
All inputs are finite; a program needn't handle non-finite values.
Results may differ from the reference program's by a relative error of at most 0.001.
Values sent between devices are 32-bit elements; how exact they have to be, the bound alone decides.
A program may use at most 64 MiB of HBM per device.

```python
import math
import jax
import jax.numpy as jnp
from jax import lax

D = 8192
STREAMS = 4
BALANCE_ROUNDS = 6
TOK_DEV = 256
TOKENS = 16384
N_DP = 64


def draw_streams(key, part):
    subkeys = jax.random.split(jax.random.fold_in(key, 7), 3)
    row_scale = jnp.exp(jax.random.uniform(subkeys[0], (TOKENS, 1, 1), minval=math.log(0.3), maxval=math.log(3.0)))
    feature_ramp = jnp.arange(D, dtype=jnp.float32) / D
    col_scale = jnp.exp(jax.random.uniform(subkeys[1], (1, STREAMS, D), minval=math.log(0.3), maxval=math.log(3.0))) * 3.0 ** feature_ramp / math.sqrt(3.0)
    base_draw = jnp.clip(jax.random.normal(subkeys[2], (TOKENS, STREAMS, D)), -6.0, 6.0)
    return (base_draw * row_scale * col_scale).astype(jnp.bfloat16)


def steps_of(own_key, extent, shards, least, largest):
    def one(position, blocks):
        draws = jax.random.uniform(jax.random.fold_in(jax.random.fold_in(own_key, 6), position), (blocks,), jnp.float32, least / len(shards), largest / len(shards))
        return jnp.repeat(jnp.exp(draws), extent[position] // blocks).reshape((-1,) + (1,) * (len(extent) - position - 1))

    factor_of = one(*shards[0])
    for cut in shards[1:]:
        factor_of = factor_of * one(*cut)
    return factor_of


def noise(own_key, shape, spread, reach, shards=(), held_as=jnp.bfloat16):
    array = spread * jax.random.normal(own_key, shape, jnp.float32)
    if shards:
        array = array * steps_of(own_key, shape, shards, -0.22, 0.18)
    return jnp.clip(array, -reach, reach).astype(held_as)


def setup_inputs(seed: int = 0) -> dict:
    keys = jax.random.split(jax.random.key(seed), 8)
    return {
        "streams": draw_streams(jax.random.fold_in(keys[7], 71), 0),
        "branch_out": noise(keys[1], (TOKENS, D), 1.0, 6.0, ((0, 64), (1, 4))),
        "merge_weight": noise(keys[2], (20, STREAMS, D), (STREAMS * D) ** -0.5, 0.03125, ((2, 256),), jnp.float32),
        "next_weight": noise(keys[3], (24, STREAMS, D), (STREAMS * D) ** -0.5, 0.03125, ((2, 256),), jnp.float32),
        "blend_bias": noise(keys[4], (44,), 1.0, 3.0, (), jnp.float32),
        "blend_scale": jnp.clip(jnp.exp(jax.random.uniform(keys[5], (5,), jnp.float32, math.log(0.5), math.log(3.0))), 0.5, 3.0),
        "norm_gain": jnp.clip(1.0 + 0.1 * jax.random.normal(keys[6], (D,), jnp.float32), 0.5, 1.5),
    }


epsilon = 1e-06

def balance_normalize(balanced_matrix):
    for balance_round in range(BALANCE_ROUNDS):
        balanced_matrix = balanced_matrix / lax.optimization_barrier(jnp.sum(balanced_matrix, axis=2, keepdims=True))
        balanced_matrix = balanced_matrix / lax.optimization_barrier(jnp.sum(balanced_matrix, axis=1, keepdims=True))
    return balanced_matrix

def logits_of(widened, weight):
    squares = lax.optimization_barrier(jnp.sum(widened * widened, axis=(1, 2)))
    rms_root = jnp.sqrt(squares / (STREAMS * D) + epsilon)
    raw_part = jnp.einsum('tic,kic->tk', widened, weight, precision=lax.Precision.HIGHEST)
    return raw_part / rms_root[:, None]

def layer_block(block_streams, block_branch, merge_weight, next_weight, blend_bias, blend_scale, norm_gain):
    widened = block_streams.astype(jnp.float32)
    score_logits = logits_of(widened, merge_weight)
    post_mix = 2.0 * jax.nn.sigmoid(blend_scale[0] * score_logits[:, :4] + blend_bias[:4])
    residual_blend = balance_normalize(jnp.exp(blend_scale[1] * score_logits[:, 4:20].reshape(-1, 4, 4) + blend_bias[4:20].reshape(4, 4)))
    mixed = jnp.einsum('tji,tic->tjc', residual_blend, widened, precision=lax.Precision.HIGHEST)
    mixed = mixed + post_mix[:, :, None] * block_branch.astype(jnp.float32)[:, None, :]
    merged_out = mixed.astype(jnp.bfloat16)
    following_logits = logits_of(mixed, next_weight)
    pre_next = jax.nn.sigmoid(blend_scale[2] * following_logits[:, :4] + blend_bias[20:24])
    post_next = 2.0 * jax.nn.sigmoid(blend_scale[3] * following_logits[:, 4:8] + blend_bias[24:28])
    residual_following = balance_normalize(jnp.exp(blend_scale[4] * following_logits[:, 8:24].reshape(-1, 4, 4) + blend_bias[28:44].reshape(4, 4)))
    united = jnp.einsum('ti,tic->tc', pre_next, mixed, precision=lax.Precision.HIGHEST)
    united_sq = lax.optimization_barrier(jnp.sum(united * united, axis=1))
    branch_in = (united / jnp.sqrt(united_sq / D + epsilon)[:, None] * norm_gain).astype(jnp.bfloat16)
    next_mix = jnp.concatenate([post_next, residual_following.reshape(-1, 16)], axis=1)
    return (merged_out, branch_in, next_mix)

def reference(streams, branch_out, merge_weight, next_weight, blend_bias, blend_scale, norm_gain):
    stacked = streams.reshape(N_DP, TOK_DEV, STREAMS, D)
    branch_blocks = branch_out.reshape(N_DP, TOK_DEV, D)

    def one_block(pair):
        return layer_block(pair[0], pair[1], merge_weight, next_weight, blend_bias, blend_scale, norm_gain)
    merged_out, branch_in, next_mix = lax.map(one_block, (stacked, branch_blocks))
    return (merged_out.reshape(TOKENS, STREAMS, D), branch_in.reshape(TOKENS, D), next_mix.reshape(TOKENS, 20))
```

```python
import jax
import jax.numpy as jnp
from jax import lax
from jax.experimental import pallas as pl
from jax.experimental.pallas import tpu as pltpu
from jax.sharding import PartitionSpec as P

D = 8192
STREAMS = 4
BALANCE_ROUNDS = 6
EPS = 1e-06

NZ = 8
NP = 8
NDP = NZ * NP
NMP = 4
TOK = 256
FEAT = 2048
TB = 32
NB = TOK // TB
SR = TB * STREAMS
XR = SR + TB
K = 24
MESH = pl.DeviceIdType.MESH
F32 = jnp.float32
BF16 = jnp.bfloat16

NT = (((1,), (1,)), ((), ()))
NN = (((1,), (0,)), ((), ()))


def dot(a, b, dims):
    return lax.dot_general(a, b, dims, preferred_element_type=F32)


def iota(shape, dim):
    return lax.broadcasted_iota(jnp.int32, shape, dim)


def split2(x):
    hi = x.astype(BF16).astype(F32)
    return [hi, x - hi]


def split3(x):
    hi = x.astype(BF16).astype(F32)
    rest = x - hi
    mid = rest.astype(BF16).astype(F32)
    return [hi, mid, rest - mid]


def pieces(parts):
    return jnp.concatenate(parts, axis=0).astype(BF16)


def token_of(u):
    return jnp.where(u < SR, u >> 2, jnp.where(u < XR, u - SR, -1))


def part_of(u):
    return jnp.where(u < SR, u & 3, STREAMS)


def block_rows(sb, bb, b):
    s3 = sb.reshape(16, TOK * STREAMS, 128)
    rows = pl.ds(pl.multiple_of(b * SR, SR), SR)
    brows = pl.ds(pl.multiple_of(b * TB, TB), TB)
    return s3, rows, brows


def balance(m):
    first = True
    for _ in range(BALANCE_ROUNDS):
        for j in range(4):
            total = (m[j][0] + m[j][1]) + (m[j][2] + m[j][3])
            if first:
                m[j] = [v / total for v in m[j]]
            else:
                inv = 1.0 / total
                m[j] = [v * inv for v in m[j]]
        first = False
        invs = [1.0 / ((m[0][i] + m[1][i]) + (m[2][i] + m[3][i])) for i in range(4)]
        m = [[m[j][i] * invs[i] for i in range(4)] for j in range(4)]
    return m


def gram_row(gt, a, b):
    a, b = min(a, b), max(a, b)
    row = b * (b + 1) // 2 + a
    return gt[row : row + 1, :]


def spread(rows5, rep5):
    d = dot(pieces(split2(rows5)), rep5[...], NN)
    part = part_of(iota((8, NB * 256), 1) & 255)
    out = []
    for base in (0, 40):
        v = d[base + 32 : base + 40]
        for a in range(4):
            v = jnp.where(part == a, d[base + 8 * a : base + 8 * a + 8], v)
        out.append(v)
    return out


def gather_kernel(
    s_hbm, b_hbm, w0_hbm, w1_hbm, bias, scale,
    sb, bb, ob, tot1, gt, cf, rep5,
    g, pacc, pbacc, rep4, w0v, w1v, gr, aexp, ex, exg, tot0,
    in_sem, ps, pr, rs, rr, es, er,
):
    dp = lax.axis_index("dp")
    mp = lax.axis_index("mp")
    z = dp // NP
    p = dp % NP
    up = lax.rem(z + 1, NZ)
    down = lax.rem(z + NZ - 1, NZ)

    def dev(d, m):
        return {"dp": d, "mp": m}

    wcopies = [
        pltpu.make_async_copy(w0_hbm, w0v, in_sem.at[0]),
        pltpu.make_async_copy(w1_hbm, w1v, in_sem.at[1]),
    ]
    for c in wcopies:
        c.start()
    icopies = [pltpu.make_async_copy(b_hbm, bb, in_sem.at[2])]
    for q in range(16):
        icopies.append(
            pltpu.make_async_copy(
                s_hbm.at[:, :, pl.ds(q * 128, 128)], sb.at[q], in_sem.at[3 + q]
            )
        )

    barrier = pltpu.get_barrier_semaphore()
    for o in range(1, NP):
        pl.semaphore_signal(
            barrier, inc=1, device_id=dev(z * NP + lax.rem(p + o, NP), mp), device_id_type=MESH
        )
    for zz in (up, down):
        pl.semaphore_signal(barrier, inc=1, device_id=dev(zz * NP + p, mp), device_id_type=MESH)
    for o in range(1, NMP):
        pl.semaphore_signal(
            barrier, inc=1, device_id=dev(dp, lax.rem(mp + o, NMP)), device_id_type=MESH
        )
    for c in icopies:
        c.start()

    for c in wcopies:
        c.wait()
    for i in range(STREAMS):
        g[0, dp, 0:20, 32 * i : 32 * i + 32] = w0v[:, i, :]
        g[1, dp, :, 32 * i : 32 * i + 32] = w1v[:, i, :]
    g[0, dp, 20:24, :] = jnp.zeros((4, 128), F32)
    pl.semaphore_wait(barrier, (NP - 1) + 2 + (NMP - 1))

    def plane(w, o, target, src):
        return pltpu.make_async_remote_copy(
            src_ref=g.at[w, src], dst_ref=g.at[w, src],
            send_sem=ps.at[w, o - 1], recv_sem=pr.at[w, o - 1],
            device_id=dev(z * NP + target, mp), device_id_type=MESH,
        )

    for w in range(2):
        for o in range(1, NP):
            plane(w, o, lax.rem(p + o, NP), dp).start()

    def hop(w, k, right, slab):
        idx = 0 if right else 1
        first = slab * NP
        ref = g.at[w, pl.ds(first, NP)]
        return pltpu.make_async_remote_copy(
            src_ref=ref, dst_ref=ref,
            send_sem=rs.at[idx, w, k - 1], recv_sem=rr.at[idx, w, k - 1],
            device_id=dev((up if right else down) * NP + p, mp), device_id_type=MESH,
        )

    def half_hop(w, right, slab):
        idx = 0 if right else 1
        first = slab * NP + (0 if right else NP // 2)
        ref = g.at[w, pl.ds(first, NP // 2)]
        return pltpu.make_async_remote_copy(
            src_ref=ref, dst_ref=ref,
            send_sem=rs.at[idx, w, 3], recv_sem=rr.at[idx, w, 3],
            device_id=dev((up if right else down) * NP + p, mp), device_id_type=MESH,
        )

    def exchange(ref, e, o, to, slot):
        return pltpu.make_async_remote_copy(
            src_ref=ref.at[slot], dst_ref=ref.at[slot],
            send_sem=es.at[e, o - 1], recv_sem=er.at[e, o - 1],
            device_id=dev(dp, to), device_id_type=MESH,
        )

    def exchange_start(ref, e):
        for o in range(1, NMP):
            exchange(ref, e, o, lax.rem(mp + o, NMP), mp).start()

    def exchange_wait(ref, e):
        for o in range(1, NMP):
            exchange(ref, e, o, lax.rem(mp + o, NMP), lax.rem(mp + NMP - o, NMP)).wait_recv()

    def plane_wait(w):
        for o in range(1, NP):
            plane(w, o, lax.rem(p + o, NP), z * NP + lax.rem(p + NP - o, NP)).wait_recv()

    tok = iota((TOK, TOK * STREAMS), 0)
    rep4[...] = jnp.where(tok == (iota((TOK, TOK * STREAMS), 1) >> 2), 1.0, 0.0).astype(BF16)
    for b in range(NB):
        u = iota((TOK, 256), 1)
        rep5[:, 256 * b : 256 * b + 256] = jnp.where(
            (iota((TOK, 256), 0) == b * TB + token_of(u)) & (u < XR), 1.0, 0.0
        ).astype(BF16)
    pacc[...] = jnp.zeros_like(pacc)
    pbacc[...] = jnp.zeros_like(pbacc)
    gr[...] = jnp.zeros_like(gr)
    for c in icopies:
        c.wait()

    plane_wait(0)
    hop(0, 1, True, z).start()
    hop(0, 1, False, z).start()
    plane_wait(1)
    hop(1, 1, True, z).start()
    hop(1, 1, False, z).start()

    def gram_block(b, carry):
        s3, rows, brows = block_rows(sb, bb, b)
        x = jnp.concatenate(
            [jnp.concatenate([s3[q, rows, :] for q in range(16)], axis=1), bb[brows, :]], axis=0
        )
        m = dot(x, x, NT)
        same = token_of(iota((XR, XR), 0)) == token_of(iota((XR, XR), 1))
        m = jnp.where(same, m, 0.0)
        top = jnp.sum(m[:SR].reshape(SR // 8, 8, XR), axis=0)
        low = jnp.sum(m[SR:], axis=0, keepdims=True)
        at = pl.multiple_of(b * 256, 256)
        gr[0:4, pl.ds(at, XR)] = top[0:4] + top[4:8]
        gr[4:5, pl.ds(at, XR)] = low
        return carry

    lax.fori_loop(0, NB, gram_block, 0)
    lanes5 = iota((8, NB * 256), 1) & 255
    part5 = part_of(lanes5)
    grv = gr[...]
    masked = [jnp.where(part5 == a, grv, 0.0) for a in range(5)]
    sums = dot(pieces(split3(jnp.concatenate(masked, axis=0))), rep5[...], NT)
    sums = sums[0:40] + sums[40:80] + sums[80:120]
    for b in range(5):
        row = b * (b + 1) // 2
        exg[mp, row : row + b + 1, :] = sums[8 * b : 8 * b + b + 1]
    exg[mp, 15:16, :] = jnp.zeros((1, TOK), F32)
    exchange_start(exg, 0)

    lane4 = iota((K, 128), 1) >> 5

    def weigh(w, slab):
        v = g[w, pl.ds(slab * NP, NP)]
        halves = []
        for h in range(2):
            a = [v[4 * h + d] for d in range(4)]
            odd = (lane4 & 1) == 1
            upper = lane4 >= 2
            st = []
            for c in (0, 2):
                st.append(jnp.where(odd, pltpu.roll(a[c + 1], 32, 1), a[c]))
                st.append(jnp.where(odd, a[c + 1], pltpu.roll(a[c], 96, 1)))
            out = [None] * 4
            for c in (0, 1):
                out[c] = jnp.where(upper, pltpu.roll(st[c + 2], 64, 1), st[c])
                out[c + 2] = jnp.where(upper, st[c + 2], pltpu.roll(st[c], 64, 1))
            halves.append(out)
        u = jnp.concatenate(
            [jnp.concatenate([halves[0][i], halves[1][i]], axis=1) for i in range(4)], axis=0
        )
        uu = pieces(split2(u))
        s3 = sb.reshape(16, TOK * STREAMS, 128)
        x = jnp.concatenate([s3[2 * slab], s3[2 * slab + 1]], axis=1)
        d = dot(uu, x, NT)
        pacc[w] += d[:96] + d[96:]
        xb = bb[:, pl.ds(pl.multiple_of(slab * 256, 256), 256)]
        d = dot(uu, xb, NT)
        pbacc[w] += d[:96] + d[96:]

    def own(w, carry):
        weigh(w, z)
        return carry

    lax.fori_loop(0, 2, own, 0)

    def step(m, carry):
        k = 1 + m // 2
        w = m % 2
        before = lax.rem(z + NZ - k, NZ)
        after = lax.rem(z + k, NZ)
        hop(w, k, True, before).wait_recv()

        @pl.when(k < 3)
        def _():
            hop(w, k + 1, True, before).start()

        @pl.when(k == 3)
        def _():
            half_hop(w, True, before).start()

        hop(w, k, False, after).wait_recv()

        @pl.when(k < 3)
        def _():
            hop(w, k + 1, False, after).start()

        @pl.when(k == 3)
        def _():
            half_hop(w, False, after).start()

        def side(n, c):
            weigh(w, lax.rem(z + NZ - k + n * 2 * k, NZ))
            return c

        lax.fori_loop(0, 2, side, 0)
        return carry

    lax.fori_loop(0, 6, step, 0)

    far = lax.rem(z + NZ // 2, NZ)

    def last(w):
        half_hop(w, True, far).wait_recv()
        half_hop(w, False, far).wait_recv()
        weigh(w, far)

    def by_token(v):
        s = dot(pieces(split3(v)), rep4[...], NT)
        return s[0:K] + s[K : 2 * K] + s[2 * K : 3 * K]

    last(0)
    ll = iota((K, TOK * STREAMS), 1) & 3
    sel = pacc[0, 72:96]
    for i in range(3):
        sel = jnp.where(ll == i, pacc[0, 24 * i : 24 * i + 24], sel)
    ex[0, mp] = by_token(sel)
    exchange_start(ex.at[0], 1)
    last(1)

    exchange_wait(exg, 0)
    gt[...] = (exg[0] + exg[1]) + (exg[2] + exg[3])
    exchange_wait(ex.at[0], 1)
    tot0[...] = (ex[0, 0] + ex[0, 1]) + (ex[0, 2] + ex[0, 3])

    sq0 = gram_row(gt, 0, 0) + gram_row(gt, 1, 1) + gram_row(gt, 2, 2) + gram_row(gt, 3, 3)
    inv0 = 1.0 / jnp.sqrt(sq0 / (STREAMS * D) + EPS)

    def logit(k):
        return tot0[k : k + 1, :] * inv0

    post = [2.0 * jax.nn.sigmoid(scale[0] * logit(j) + bias[j]) for j in range(4)]
    res = balance(
        [
            [jnp.exp(scale[1] * logit(4 + 4 * j + i) + bias[4 + 4 * j + i]) for i in range(4)]
            for j in range(4)
        ]
    )
    co = [[res[j][0], res[j][1], res[j][2], res[j][3], post[j]] for j in range(4)]
    for a in range(5):
        for j in range(4):
            cf[8 * a + j : 8 * a + j + 1, :] = co[j][a]
            cf[8 * a + 4 + j : 8 * a + 5 + j, :] = co[j][a]
    hi, lo = spread(cf[...], rep5)
    aexp[0] = hi
    aexp[1] = lo

    both = hi + lo
    rexp = jnp.concatenate([both[:, 256 * b : 256 * b + 128] for b in range(NB)], axis=1)
    acc = rexp[0:1] * pacc[1, 0:24]
    for j in range(1, 4):
        acc = acc + rexp[j : j + 1] * pacc[1, 24 * j : 24 * j + 24]
    raw1 = by_token(acc)
    for j in range(4):
        raw1 = raw1 + post[j] * pbacc[1, 24 * j : 24 * j + 24]
    ex[1, mp] = raw1
    exchange_start(ex.at[1], 2)

    tl = token_of(iota((SR, XR), 1))
    tr = iota((SR, XR), 0) >> 2

    def mix_block(b, carry):
        s3, rows, brows = block_rows(sb, bb, b)
        o3 = ob.reshape(16, TOK * STREAMS, 128)
        at = pl.multiple_of(b * 256, 256)
        parts = []
        for n in range(2):
            v = aexp[n, :, pl.ds(at, 256)]
            full = jnp.concatenate([v] * (SR // 8), axis=0)[:, :XR]
            parts.append(jnp.where(tl == tr, full, 0.0))
        amat = pieces(parts)
        for f in range(8):
            x = jnp.concatenate(
                [
                    jnp.concatenate([s3[2 * f, rows, :], s3[2 * f + 1, rows, :]], axis=1),
                    bb[brows, 256 * f : 256 * f + 256],
                ],
                axis=0,
            )
            d = dot(amat, x, NN)
            d = (d[:SR] + d[SR:]).astype(BF16)
            o3[2 * f, rows, :] = d[:, :128]
            o3[2 * f + 1, rows, :] = d[:, 128:]
        return carry

    lax.fori_loop(0, NB, mix_block, 0)

    exchange_wait(ex.at[1], 2)
    tot1[...] = (ex[1, 0] + ex[1, 1]) + (ex[1, 2] + ex[1, 3])

    for w in range(2):
        for o in range(1, NP):
            plane(w, o, lax.rem(p + o, NP), dp).wait_send()
        for right in (True, False):
            for k in range(1, 4):
                hop(w, k, right, z).wait_send()
            half_hop(w, right, z).wait_send()
    for e, ref in ((0, exg), (1, ex.at[0]), (2, ex.at[1])):
        for o in range(1, NMP):
            exchange(ref, e, o, lax.rem(mp + o, NMP), mp).wait_send()


def finish_kernel(
    sb, bb, ob, tot1, gt, cf, rep5, gain, bias, scale,
    streams_out, branch_in, mix, qexp, nm, obuf, osem, bsem,
):
    outs = [
        pltpu.make_async_copy(ob.at[q], streams_out.at[:, :, pl.ds(q * 128, 128)], osem.at[q])
        for q in range(16)
    ]
    for c in outs:
        c.start()

    a = [[cf[8 * n + j : 8 * n + j + 1, :] for n in range(5)] for j in range(4)]
    sq1 = jnp.zeros((1, TOK), F32)
    for m in range(5):
        for n in range(m, 5):
            s = (a[0][m] * a[0][n] + a[1][m] * a[1][n]) + (a[2][m] * a[2][n] + a[3][m] * a[3][n])
            sq1 = sq1 + (1.0 if m == n else 2.0) * s * gram_row(gt, m, n)
    inv1 = 1.0 / jnp.sqrt(jnp.maximum(sq1, 0.0) / (STREAMS * D) + EPS)

    def logit(k):
        return tot1[k : k + 1, :] * inv1

    pre = [jax.nn.sigmoid(scale[2] * logit(j) + bias[20 + j]) for j in range(4)]
    q = [
        (pre[0] * a[0][n] + pre[1] * a[1][n]) + (pre[2] * a[2][n] + pre[3] * a[3][n])
        for n in range(5)
    ]
    usq = jnp.zeros((1, TOK), F32)
    for m in range(5):
        for n in range(m, 5):
            usq = usq + (1.0 if m == n else 2.0) * (q[m] * q[n]) * gram_row(gt, m, n)
    norm = 1.0 / jnp.sqrt(jnp.maximum(usq, 0.0) / D + EPS)
    q8 = jnp.concatenate([jnp.broadcast_to(v * norm, (8, TOK)) for v in q], axis=0)
    hi, lo = spread(q8, rep5)
    qexp[0] = hi
    qexp[1] = lo

    tl = token_of(iota((TB, XR), 1))
    tr = iota((TB, XR), 0)

    def out_copy(b):
        rows = pl.ds(pl.multiple_of(b * TB, TB), TB)
        return pltpu.make_async_copy(obuf.at[rows], branch_in.at[rows], bsem.at[b])

    def unite_block(b, carry):
        s3, rows, brows = block_rows(sb, bb, b)
        at = pl.multiple_of(b * 256, 256)
        parts = []
        for n in range(2):
            v = qexp[n, :, pl.ds(at, 256)]
            full = jnp.concatenate([v] * (TB // 8), axis=0)[:, :XR]
            parts.append(jnp.where(tl == tr, full, 0.0))
        qmat = pieces(parts)
        for f in range(8):
            x = jnp.concatenate(
                [
                    jnp.concatenate([s3[2 * f, rows, :], s3[2 * f + 1, rows, :]], axis=1),
                    bb[brows, 256 * f : 256 * f + 256],
                ],
                axis=0,
            )
            d = dot(qmat, x, NN)
            d = (d[:TB] + d[TB:]) * gain[0:1, 256 * f : 256 * f + 256]
            obuf[brows, 256 * f : 256 * f + 256] = d.astype(BF16)
        out_copy(b).start()
        return carry

    lax.fori_loop(0, NB, unite_block, 0)

    post = [2.0 * jax.nn.sigmoid(scale[3] * logit(4 + j) + bias[24 + j]) for j in range(4)]
    res = balance(
        [
            [jnp.exp(scale[4] * logit(8 + 4 * j + i) + bias[28 + 4 * j + i]) for i in range(4)]
            for j in range(4)
        ]
    )
    for j in range(4):
        nm[j : j + 1, :] = post[j]
        for i in range(4):
            nm[4 + 4 * j + i : 5 + 4 * j + i, :] = res[j][i]
    nm[20:128, :] = jnp.zeros((108, TOK), F32)
    mix[...] = jnp.transpose(nm[...])[:, :20]

    def drain(b, carry):
        out_copy(b).wait()
        return carry

    lax.fori_loop(0, NB, drain, 0)
    for c in outs:
        c.wait()


def local(streams, branch_out, merge_weight, next_weight, blend_bias, blend_scale, norm_gain):
    vmem = pl.BlockSpec(memory_space=pltpu.VMEM)
    smem = pl.BlockSpec(memory_space=pltpu.SMEM)
    hbm = pl.BlockSpec(memory_space=pltpu.HBM)
    kept = (
        pltpu.VMEM((16, TOK, STREAMS, 128), BF16),
        pltpu.VMEM((TOK, FEAT), BF16),
        pltpu.VMEM((16, TOK, STREAMS, 128), BF16),
        pltpu.VMEM((K, TOK), F32),
        pltpu.VMEM((16, TOK), F32),
        pltpu.VMEM((40, TOK), F32),
        pltpu.VMEM((TOK, NB * 256), BF16),
    )
    dma = pltpu.SemaphoreType.DMA
    state = pl.pallas_call(
        gather_kernel,
        out_shape=kept,
        in_specs=[hbm, hbm, hbm, hbm, smem, smem],
        out_specs=(vmem,) * 7,
        scratch_shapes=[
            pltpu.VMEM((2, NDP, K, 128), F32),
            pltpu.VMEM((2, 4 * K, TOK * STREAMS), F32),
            pltpu.VMEM((2, 4 * K, TOK), F32),
            pltpu.VMEM((TOK, TOK * STREAMS), BF16),
            pltpu.VMEM((20, STREAMS, 32), F32),
            pltpu.VMEM((24, STREAMS, 32), F32),
            pltpu.VMEM((8, NB * 256), F32),
            pltpu.VMEM((2, 8, NB * 256), F32),
            pltpu.VMEM((2, NMP, K, TOK), F32),
            pltpu.VMEM((NMP, 16, TOK), F32),
            pltpu.VMEM((K, TOK), F32),
            dma((19,)),
            dma((2, NP - 1)),
            dma((2, NP - 1)),
            dma((2, 2, 4)),
            dma((2, 2, 4)),
            dma((3, NMP - 1)),
            dma((3, NMP - 1)),
        ],
        compiler_params=pltpu.CompilerParams(
            collective_id=0, has_side_effects=True, vmem_limit_bytes=24 << 20
        ),
        name="gather_mix",
    )(streams, branch_out, merge_weight, next_weight, blend_bias, blend_scale)
    return pl.pallas_call(
        finish_kernel,
        out_shape=(
            jax.ShapeDtypeStruct((TOK, STREAMS, FEAT), BF16),
            jax.ShapeDtypeStruct((TOK, FEAT), BF16),
            jax.ShapeDtypeStruct((TOK, 20), F32),
        ),
        in_specs=[vmem] * 8 + [smem, smem],
        out_specs=(hbm, hbm, vmem),
        scratch_shapes=[
            pltpu.VMEM((2, 8, NB * 256), F32),
            pltpu.VMEM((128, TOK), F32),
            pltpu.VMEM((TOK, FEAT), BF16),
            dma((16,)),
            dma((NB,)),
        ],
        compiler_params=pltpu.CompilerParams(vmem_limit_bytes=16 << 20),
        name="finish",
    )(*state, norm_gain.reshape(1, FEAT), blend_bias, blend_scale)


def solution(mesh):
    placed = (
        P("dp", None, "mp"),
        P("dp", "mp"),
        P(None, None, ("mp", "dp")),
        P(None, None, ("mp", "dp")),
        P(),
        P(),
        P("mp"),
    )
    return jax.shard_map(
        local,
        mesh=mesh,
        in_specs=placed,
        out_specs=(P("dp", None, "mp"), P("dp", "mp"), P("dp", None)),
        check_vma=False,
    )
```

```python
import jax
import jax.numpy as jnp
from jax import lax
from jax.experimental import pallas as pl
from jax.experimental.pallas import tpu as pltpu
from jax.sharding import PartitionSpec as P

D = 8192
STREAMS = 4
BALANCE_ROUNDS = 6
EPS = 1e-06

NZ = 8
NP = 8
NDP = NZ * NP
NMP = 4
TOK = 256
FEAT = 2048
TB = 32
NB = TOK // TB
SR = TB * STREAMS
XR = SR + TB
K = 24
MESH = pl.DeviceIdType.MESH
F32 = jnp.float32
BF16 = jnp.bfloat16

NT = (((1,), (1,)), ((), ()))
NN = (((1,), (0,)), ((), ()))


def dot(a, b, dims):
    return lax.dot_general(a, b, dims, preferred_element_type=F32)


def iota(shape, dim):
    return lax.broadcasted_iota(jnp.int32, shape, dim)


def split2(x):
    hi = x.astype(BF16).astype(F32)
    return [hi, x - hi]


def split3(x):
    hi = x.astype(BF16).astype(F32)
    rest = x - hi
    mid = rest.astype(BF16).astype(F32)
    return [hi, mid, rest - mid]


def pieces(parts):
    return jnp.concatenate(parts, axis=0).astype(BF16)


def token_of(u):
    return jnp.where(u < SR, u >> 2, jnp.where(u < XR, u - SR, -1))


def part_of(u):
    return jnp.where(u < SR, u & 3, STREAMS)


def block_rows(sb, bb, b):
    s3 = sb.reshape(16, TOK * STREAMS, 128)
    rows = pl.ds(pl.multiple_of(b * SR, SR), SR)
    brows = pl.ds(pl.multiple_of(b * TB, TB), TB)
    return s3, rows, brows


def balance(m):
    first = True
    for _ in range(BALANCE_ROUNDS):
        for j in range(4):
            total = (m[j][0] + m[j][1]) + (m[j][2] + m[j][3])
            if first:
                m[j] = [v / total for v in m[j]]
            else:
                inv = 1.0 / total
                m[j] = [v * inv for v in m[j]]
        first = False
        invs = [1.0 / ((m[0][i] + m[1][i]) + (m[2][i] + m[3][i])) for i in range(4)]
        m = [[m[j][i] * invs[i] for i in range(4)] for j in range(4)]
    return m


def gram_row(gt, a, b):
    a, b = min(a, b), max(a, b)
    row = b * (b + 1) // 2 + a
    return gt[row : row + 1, :]


def spread(rows5, rep5):
    d = dot(pieces(split2(rows5)), rep5[...], NN)
    part = part_of(iota((8, NB * 256), 1) & 255)
    out = []
    for base in (0, 40):
        v = d[base + 32 : base + 40]
        for a in range(4):
            v = jnp.where(part == a, d[base + 8 * a : base + 8 * a + 8], v)
        out.append(v)
    return out


def gather_kernel(
    s_hbm, b_hbm, w0_hbm, w1_hbm, bias_hbm, scale_hbm,
    sb, bb, ob, tot1, gt, cf, rep5,
    g, pacc, pbacc, rep4, w0v, w1v, gr, aexp, ex, exg, tot0, bias, scale,
    in_sem, ps, pr, rs, rr, es, er,
):
    dp = lax.axis_index("dp")
    mp = lax.axis_index("mp")
    z = dp // NP
    p = dp % NP
    up = lax.rem(z + 1, NZ)
    down = lax.rem(z + NZ - 1, NZ)

    def dev(d, m):
        return {"dp": d, "mp": m}

    wcopies = [
        pltpu.make_async_copy(w0_hbm, w0v, in_sem.at[0]),
        pltpu.make_async_copy(w1_hbm, w1v, in_sem.at[1]),
    ]
    scopies = [
        pltpu.make_async_copy(bias_hbm, bias, in_sem.at[19]),
        pltpu.make_async_copy(scale_hbm, scale, in_sem.at[20]),
    ]
    for c in wcopies:
        c.start()
    icopies = [pltpu.make_async_copy(b_hbm, bb, in_sem.at[2])]
    for q in range(16):
        icopies.append(
            pltpu.make_async_copy(
                s_hbm.at[:, :, pl.ds(q * 128, 128)], sb.at[q], in_sem.at[3 + q]
            )
        )

    barrier = pltpu.get_barrier_semaphore()
    for o in range(1, NP):
        pl.semaphore_signal(
            barrier, inc=1, device_id=dev(z * NP + lax.rem(p + o, NP), mp), device_id_type=MESH
        )
    for zz in (up, down):
        pl.semaphore_signal(barrier, inc=1, device_id=dev(zz * NP + p, mp), device_id_type=MESH)
    for o in range(1, NMP):
        pl.semaphore_signal(
            barrier, inc=1, device_id=dev(dp, lax.rem(mp + o, NMP)), device_id_type=MESH
        )
    for c in icopies + scopies:
        c.start()

    for c in wcopies:
        c.wait()
    for i in range(STREAMS):
        g[0, dp, 0:20, 32 * i : 32 * i + 32] = w0v[:, i, :]
        g[1, dp, :, 32 * i : 32 * i + 32] = w1v[:, i, :]
    g[0, dp, 20:24, :] = jnp.zeros((4, 128), F32)
    pl.semaphore_wait(barrier, (NP - 1) + 2 + (NMP - 1))

    def plane(w, o, target, src):
        return pltpu.make_async_remote_copy(
            src_ref=g.at[w, src], dst_ref=g.at[w, src],
            send_sem=ps.at[w, o - 1], recv_sem=pr.at[w, o - 1],
            device_id=dev(z * NP + target, mp), device_id_type=MESH,
        )

    for w in range(2):
        for o in range(1, NP):
            plane(w, o, lax.rem(p + o, NP), dp).start()

    def hop(w, k, right, slab):
        idx = 0 if right else 1
        first = slab * NP
        ref = g.at[w, pl.ds(first, NP)]
        return pltpu.make_async_remote_copy(
            src_ref=ref, dst_ref=ref,
            send_sem=rs.at[idx, w, k - 1], recv_sem=rr.at[idx, w, k - 1],
            device_id=dev((up if right else down) * NP + p, mp), device_id_type=MESH,
        )

    def half_hop(w, right, slab):
        idx = 0 if right else 1
        first = slab * NP + (0 if right else NP // 2)
        ref = g.at[w, pl.ds(first, NP // 2)]
        return pltpu.make_async_remote_copy(
            src_ref=ref, dst_ref=ref,
            send_sem=rs.at[idx, w, 3], recv_sem=rr.at[idx, w, 3],
            device_id=dev((up if right else down) * NP + p, mp), device_id_type=MESH,
        )

    def exchange(ref, e, o, to, slot):
        return pltpu.make_async_remote_copy(
            src_ref=ref.at[slot], dst_ref=ref.at[slot],
            send_sem=es.at[e, o - 1], recv_sem=er.at[e, o - 1],
            device_id=dev(dp, to), device_id_type=MESH,
        )

    def exchange_start(ref, e):
        for o in range(1, NMP):
            exchange(ref, e, o, lax.rem(mp + o, NMP), mp).start()

    def exchange_wait(ref, e):
        for o in range(1, NMP):
            exchange(ref, e, o, lax.rem(mp + o, NMP), lax.rem(mp + NMP - o, NMP)).wait_recv()

    def plane_wait(w):
        for o in range(1, NP):
            plane(w, o, lax.rem(p + o, NP), z * NP + lax.rem(p + NP - o, NP)).wait_recv()

    tok = iota((TOK, TOK * STREAMS), 0)
    rep4[...] = jnp.where(tok == (iota((TOK, TOK * STREAMS), 1) >> 2), 1.0, 0.0).astype(BF16)
    for b in range(NB):
        u = iota((TOK, 256), 1)
        rep5[:, 256 * b : 256 * b + 256] = jnp.where(
            (iota((TOK, 256), 0) == b * TB + token_of(u)) & (u < XR), 1.0, 0.0
        ).astype(BF16)
    pacc[...] = jnp.zeros_like(pacc)
    pbacc[...] = jnp.zeros_like(pbacc)
    gr[...] = jnp.zeros_like(gr)
    for c in icopies + scopies:
        c.wait()

    plane_wait(0)
    hop(0, 1, True, z).start()
    hop(0, 1, False, z).start()
    plane_wait(1)
    hop(1, 1, True, z).start()
    hop(1, 1, False, z).start()

    def gram_block(b, carry):
        s3, rows, brows = block_rows(sb, bb, b)
        x = jnp.concatenate(
            [jnp.concatenate([s3[q, rows, :] for q in range(16)], axis=1), bb[brows, :]], axis=0
        )
        m = dot(x, x, NT)
        same = token_of(iota((XR, XR), 0)) == token_of(iota((XR, XR), 1))
        m = jnp.where(same, m, 0.0)
        top = jnp.sum(m[:SR].reshape(SR // 8, 8, XR), axis=0)
        low = jnp.sum(m[SR:], axis=0, keepdims=True)
        at = pl.multiple_of(b * 256, 256)
        gr[0:4, pl.ds(at, XR)] = top[0:4] + top[4:8]
        gr[4:5, pl.ds(at, XR)] = low
        return carry

    lax.fori_loop(0, NB, gram_block, 0)
    lanes5 = iota((8, NB * 256), 1) & 255
    part5 = part_of(lanes5)
    grv = gr[...]
    masked = [jnp.where(part5 == a, grv, 0.0) for a in range(5)]
    sums = dot(pieces(split3(jnp.concatenate(masked, axis=0))), rep5[...], NT)
    sums = sums[0:40] + sums[40:80] + sums[80:120]
    for b in range(5):
        row = b * (b + 1) // 2
        exg[mp, row : row + b + 1, :] = sums[8 * b : 8 * b + b + 1]
    exg[mp, 15:16, :] = jnp.zeros((1, TOK), F32)
    exchange_start(exg, 0)

    lane4 = iota((K, 128), 1) >> 5

    def weigh(w, slab):
        v = g[w, pl.ds(slab * NP, NP)]
        halves = []
        for h in range(2):
            a = [v[4 * h + d] for d in range(4)]
            odd = (lane4 & 1) == 1
            upper = lane4 >= 2
            st = []
            for c in (0, 2):
                st.append(jnp.where(odd, pltpu.roll(a[c + 1], 32, 1), a[c]))
                st.append(jnp.where(odd, a[c + 1], pltpu.roll(a[c], 96, 1)))
            out = [None] * 4
            for c in (0, 1):
                out[c] = jnp.where(upper, pltpu.roll(st[c + 2], 64, 1), st[c])
                out[c + 2] = jnp.where(upper, st[c + 2], pltpu.roll(st[c], 64, 1))
            halves.append(out)
        u = jnp.concatenate(
            [jnp.concatenate([halves[0][i], halves[1][i]], axis=1) for i in range(4)], axis=0
        )
        uu = pieces(split2(u))
        s3 = sb.reshape(16, TOK * STREAMS, 128)
        x = jnp.concatenate([s3[2 * slab], s3[2 * slab + 1]], axis=1)
        d = dot(uu, x, NT)
        pacc[w] += d[:96] + d[96:]
        xb = bb[:, pl.ds(pl.multiple_of(slab * 256, 256), 256)]
        d = dot(uu, xb, NT)
        pbacc[w] += d[:96] + d[96:]

    def own(w, carry):
        weigh(w, z)
        return carry

    lax.fori_loop(0, 2, own, 0)

    def step(m, carry):
        k = 1 + m // 2
        w = m % 2
        before = lax.rem(z + NZ - k, NZ)
        after = lax.rem(z + k, NZ)
        hop(w, k, True, before).wait_recv()

        @pl.when(k < 3)
        def _():
            hop(w, k + 1, True, before).start()

        @pl.when(k == 3)
        def _():
            half_hop(w, True, before).start()

        hop(w, k, False, after).wait_recv()

        @pl.when(k < 3)
        def _():
            hop(w, k + 1, False, after).start()

        @pl.when(k == 3)
        def _():
            half_hop(w, False, after).start()

        def side(n, c):
            weigh(w, lax.rem(z + NZ - k + n * 2 * k, NZ))
            return c

        lax.fori_loop(0, 2, side, 0)
        return carry

    lax.fori_loop(0, 6, step, 0)

    far = lax.rem(z + NZ // 2, NZ)

    def last(w):
        half_hop(w, True, far).wait_recv()
        half_hop(w, False, far).wait_recv()
        weigh(w, far)

    def by_token(v):
        s = dot(pieces(split3(v)), rep4[...], NT)
        return s[0:K] + s[K : 2 * K] + s[2 * K : 3 * K]

    last(0)
    ll = iota((K, TOK * STREAMS), 1) & 3
    sel = pacc[0, 72:96]
    for i in range(3):
        sel = jnp.where(ll == i, pacc[0, 24 * i : 24 * i + 24], sel)
    ex[0, mp] = by_token(sel)
    exchange_start(ex.at[0], 1)
    last(1)

    exchange_wait(exg, 0)
    gt[...] = (exg[0] + exg[1]) + (exg[2] + exg[3])
    exchange_wait(ex.at[0], 1)
    tot0[...] = (ex[0, 0] + ex[0, 1]) + (ex[0, 2] + ex[0, 3])

    sq0 = gram_row(gt, 0, 0) + gram_row(gt, 1, 1) + gram_row(gt, 2, 2) + gram_row(gt, 3, 3)
    inv0 = 1.0 / jnp.sqrt(sq0 / (STREAMS * D) + EPS)

    def logit(k):
        return tot0[k : k + 1, :] * inv0

    post = [2.0 * jax.nn.sigmoid(scale[0] * logit(j) + bias[j]) for j in range(4)]
    res = balance(
        [
            [jnp.exp(scale[1] * logit(4 + 4 * j + i) + bias[4 + 4 * j + i]) for i in range(4)]
            for j in range(4)
        ]
    )
    co = [[res[j][0], res[j][1], res[j][2], res[j][3], post[j]] for j in range(4)]
    for a in range(5):
        for j in range(4):
            cf[8 * a + j : 8 * a + j + 1, :] = co[j][a]
            cf[8 * a + 4 + j : 8 * a + 5 + j, :] = co[j][a]
    hi, lo = spread(cf[...], rep5)
    aexp[0] = hi
    aexp[1] = lo

    both = hi + lo
    rexp = jnp.concatenate([both[:, 256 * b : 256 * b + 128] for b in range(NB)], axis=1)
    acc = rexp[0:1] * pacc[1, 0:24]
    for j in range(1, 4):
        acc = acc + rexp[j : j + 1] * pacc[1, 24 * j : 24 * j + 24]
    raw1 = by_token(acc)
    for j in range(4):
        raw1 = raw1 + post[j] * pbacc[1, 24 * j : 24 * j + 24]
    ex[1, mp] = raw1
    exchange_start(ex.at[1], 2)

    tl = token_of(iota((SR, XR), 1))
    tr = iota((SR, XR), 0) >> 2

    def mix_block(b, carry):
        s3, rows, brows = block_rows(sb, bb, b)
        o3 = ob.reshape(16, TOK * STREAMS, 128)
        at = pl.multiple_of(b * 256, 256)
        parts = []
        for n in range(2):
            v = aexp[n, :, pl.ds(at, 256)]
            full = jnp.concatenate([v] * (SR // 8), axis=0)[:, :XR]
            parts.append(jnp.where(tl == tr, full, 0.0))
        amat = pieces(parts)
        for f in range(8):
            x = jnp.concatenate(
                [
                    jnp.concatenate([s3[2 * f, rows, :], s3[2 * f + 1, rows, :]], axis=1),
                    bb[brows, 256 * f : 256 * f + 256],
                ],
                axis=0,
            )
            d = dot(amat, x, NN)
            d = (d[:SR] + d[SR:]).astype(BF16)
            o3[2 * f, rows, :] = d[:, :128]
            o3[2 * f + 1, rows, :] = d[:, 128:]
        return carry

    lax.fori_loop(0, NB, mix_block, 0)

    exchange_wait(ex.at[1], 2)
    tot1[...] = (ex[1, 0] + ex[1, 1]) + (ex[1, 2] + ex[1, 3])

    for w in range(2):
        for o in range(1, NP):
            plane(w, o, lax.rem(p + o, NP), dp).wait_send()
        for right in (True, False):
            for k in range(1, 4):
                hop(w, k, right, z).wait_send()
            half_hop(w, right, z).wait_send()
    for e, ref in ((0, exg), (1, ex.at[0]), (2, ex.at[1])):
        for o in range(1, NMP):
            exchange(ref, e, o, lax.rem(mp + o, NMP), mp).wait_send()


def finish_kernel(
    sb, bb, ob, tot1, gt, cf, rep5, gain, bias, scale,
    streams_out, branch_in, mix, qexp, obuf, osem, bsem,
):
    outs = [
        pltpu.make_async_copy(ob.at[q], streams_out.at[:, :, pl.ds(q * 128, 128)], osem.at[q])
        for q in range(16)
    ]
    for c in outs:
        c.start()

    a = [[cf[8 * n + j : 8 * n + j + 1, :] for n in range(5)] for j in range(4)]
    sq1 = jnp.zeros((1, TOK), F32)
    for m in range(5):
        for n in range(m, 5):
            s = (a[0][m] * a[0][n] + a[1][m] * a[1][n]) + (a[2][m] * a[2][n] + a[3][m] * a[3][n])
            sq1 = sq1 + (1.0 if m == n else 2.0) * s * gram_row(gt, m, n)
    inv1 = 1.0 / jnp.sqrt(jnp.maximum(sq1, 0.0) / (STREAMS * D) + EPS)

    def logit(k):
        return tot1[k : k + 1, :] * inv1

    pre = [jax.nn.sigmoid(scale[2] * logit(j) + bias[20 + j]) for j in range(4)]
    q = [
        (pre[0] * a[0][n] + pre[1] * a[1][n]) + (pre[2] * a[2][n] + pre[3] * a[3][n])
        for n in range(5)
    ]
    usq = jnp.zeros((1, TOK), F32)
    for m in range(5):
        for n in range(m, 5):
            usq = usq + (1.0 if m == n else 2.0) * (q[m] * q[n]) * gram_row(gt, m, n)
    norm = 1.0 / jnp.sqrt(jnp.maximum(usq, 0.0) / D + EPS)
    q8 = jnp.concatenate([jnp.broadcast_to(v * norm, (8, TOK)) for v in q], axis=0)
    hi, lo = spread(q8, rep5)
    qexp[0] = hi
    qexp[1] = lo

    tl = token_of(iota((TB, XR), 1))
    tr = iota((TB, XR), 0)

    def out_copy(b):
        rows = pl.ds(pl.multiple_of(b * TB, TB), TB)
        return pltpu.make_async_copy(obuf.at[rows], branch_in.at[rows], bsem.at[b])

    def unite_block(b, carry):
        s3, rows, brows = block_rows(sb, bb, b)
        at = pl.multiple_of(b * 256, 256)
        parts = []
        for n in range(2):
            v = qexp[n, :, pl.ds(at, 256)]
            full = jnp.concatenate([v] * (TB // 8), axis=0)[:, :XR]
            parts.append(jnp.where(tl == tr, full, 0.0))
        qmat = pieces(parts)
        for f in range(8):
            x = jnp.concatenate(
                [
                    jnp.concatenate([s3[2 * f, rows, :], s3[2 * f + 1, rows, :]], axis=1),
                    bb[brows, 256 * f : 256 * f + 256],
                ],
                axis=0,
            )
            d = dot(qmat, x, NN)
            d = (d[:TB] + d[TB:]) * gain[0:1, 256 * f : 256 * f + 256]
            obuf[brows, 256 * f : 256 * f + 256] = d.astype(BF16)
        out_copy(b).start()
        return carry

    lax.fori_loop(0, NB, unite_block, 0)

    post = [2.0 * jax.nn.sigmoid(scale[3] * logit(4 + j) + bias[24 + j]) for j in range(4)]
    res = balance(
        [
            [jnp.exp(scale[4] * logit(8 + 4 * j + i) + bias[28 + 4 * j + i]) for i in range(4)]
            for j in range(4)
        ]
    )
    for j in range(4):
        mix[j : j + 1, :] = post[j]
        for i in range(4):
            mix[4 + 4 * j + i : 5 + 4 * j + i, :] = res[j][i]

    def drain(b, carry):
        out_copy(b).wait()
        return carry

    lax.fori_loop(0, NB, drain, 0)
    for c in outs:
        c.wait()


def local(streams, branch_out, merge_weight, next_weight, blend_bias, blend_scale, norm_gain):
    vmem = pl.BlockSpec(memory_space=pltpu.VMEM)
    smem = pl.BlockSpec(memory_space=pltpu.SMEM)
    hbm = pl.BlockSpec(memory_space=pltpu.HBM)
    kept = (
        pltpu.VMEM((16, TOK, STREAMS, 128), BF16),
        pltpu.VMEM((TOK, FEAT), BF16),
        pltpu.VMEM((16, TOK, STREAMS, 128), BF16),
        pltpu.VMEM((K, TOK), F32),
        pltpu.VMEM((16, TOK), F32),
        pltpu.VMEM((40, TOK), F32),
        pltpu.VMEM((TOK, NB * 256), BF16),
    )
    dma = pltpu.SemaphoreType.DMA
    given = tuple(
        pltpu.with_memory_space_constraint(v, pltpu.HBM)
        for v in (streams, branch_out, merge_weight, next_weight, blend_bias, blend_scale)
    )
    state = pl.pallas_call(
        gather_kernel,
        out_shape=kept,
        in_specs=[hbm] * 6,
        out_specs=(vmem,) * 7,
        scratch_shapes=[
            pltpu.VMEM((2, NDP, K, 128), F32),
            pltpu.VMEM((2, 4 * K, TOK * STREAMS), F32),
            pltpu.VMEM((2, 4 * K, TOK), F32),
            pltpu.VMEM((TOK, TOK * STREAMS), BF16),
            pltpu.VMEM((20, STREAMS, 32), F32),
            pltpu.VMEM((24, STREAMS, 32), F32),
            pltpu.VMEM((8, NB * 256), F32),
            pltpu.VMEM((2, 8, NB * 256), F32),
            pltpu.VMEM((2, NMP, K, TOK), F32),
            pltpu.VMEM((NMP, 16, TOK), F32),
            pltpu.VMEM((K, TOK), F32),
            pltpu.SMEM((44,), F32),
            pltpu.SMEM((5,), F32),
            dma((21,)),
            dma((2, NP - 1)),
            dma((2, NP - 1)),
            dma((2, 2, 4)),
            dma((2, 2, 4)),
            dma((3, NMP - 1)),
            dma((3, NMP - 1)),
        ],
        compiler_params=pltpu.CompilerParams(
            collective_id=0, has_side_effects=True, vmem_limit_bytes=24 << 20
        ),
        name="gather_mix",
    )(*given)
    streams_out, branch_in, mix = pl.pallas_call(
        finish_kernel,
        out_shape=(
            jax.ShapeDtypeStruct((TOK, STREAMS, FEAT), BF16),
            jax.ShapeDtypeStruct((TOK, FEAT), BF16),
            jax.ShapeDtypeStruct((20, TOK), F32),
        ),
        in_specs=[vmem] * 8 + [smem, smem],
        out_specs=(hbm, hbm, vmem),
        scratch_shapes=[
            pltpu.VMEM((2, 8, NB * 256), F32),
            pltpu.VMEM((TOK, FEAT), BF16),
            dma((16,)),
            dma((NB,)),
        ],
        compiler_params=pltpu.CompilerParams(vmem_limit_bytes=16 << 20),
        name="finish",
    )(*state, norm_gain.reshape(1, FEAT), blend_bias, blend_scale)
    return streams_out, branch_in, mix.T


def solution(mesh):
    placed = (
        P("dp", None, "mp"),
        P("dp", "mp"),
        P(None, None, ("mp", "dp")),
        P(None, None, ("mp", "dp")),
        P(),
        P(),
        P("mp"),
    )
    return jax.shard_map(
        local,
        mesh=mesh,
        in_specs=placed,
        out_specs=(P("dp", None, "mp"), P("dp", "mp"), P("dp", None)),
        check_vma=False,
    )
```
